32 devices in a mesh: tensor: 4 (over x, core), dp: 8 (over z, y).
Axes of the slice: x: 2, y: 2, z: 4, core: 2. Of those that a mesh axis runs over, the one named last changes fastest.
Arguments:
- tokens: bfloat16 [16384, 768], P('dp'), may hold values from -6 to 6
- segments: int32 [16, 1024], P('dp'), may hold values from 0 to 3, never falling along the last dimension, each value on 1 to 768 neighbouring positions
- random_blocks: int32 [16, 12, 3], P(None, 'tensor'), may hold values from 0 to 15
- w_query: bfloat16 [768, 768], P('dp', 'tensor'), may hold values from -0.21875 to 0.21875
- w_key: bfloat16 [768, 768], P('dp', 'tensor'), may hold values from -0.21875 to 0.21875
- w_value: bfloat16 [768, 768], P('dp', 'tensor'), may hold values from -0.21875 to 0.21875
- w_out: bfloat16 [768, 768], P('tensor', 'dp'), may hold values from -0.875 to 0.875
- w_up: bfloat16 [768, 3072], P('dp', 'tensor'), may hold values from -0.21875 to 0.21875
- w_down: bfloat16 [3072, 768], P('tensor', 'dp'), may hold values from -0.109375 to 0.109375
- bias_query: bfloat16 [768], P(('tensor', 'dp')), may hold values from -3 to 3
- bias_value: bfloat16 [768], P(('tensor', 'dp')), may hold values from -3 to 3
- bias_out: bfloat16 [768], P('dp'), may hold values from -3 to 3
- bias_up: bfloat16 [3072], P(('tensor', 'dp')), may hold values from -3 to 3
- bias_down: bfloat16 [768], P('dp'), may hold values from -3 to 3
- gain_attn: bfloat16 [768], P('dp'), may hold values from 0.099609375 to 1.8984375
- shift_attn: bfloat16 [768], P('dp'), may hold values from -3 to 3
- gain_out: bfloat16 [768], P('dp'), may hold values from 0.099609375 to 1.8984375
- shift_out: bfloat16 [768], P('dp'), may hold values from -3 to 3
- cotangent: bfloat16 [16384, 768], P('dp'), may hold values from -6 to 6
Outputs:
- activations: bfloat16 [16384, 768], P('dp')
- input_grad: float32 [16384, 768], P('dp')
- grad_w_query: float32 [768, 768], P('dp', 'tensor')
- grad_w_key: float32 [768, 768], P('dp', 'tensor')
- grad_w_value: float32 [768, 768], P('dp', 'tensor')
- grad_w_out: float32 [768, 768], P('tensor', 'dp')
- grad_w_up: float32 [768, 3072], P('dp', 'tensor')
- grad_w_down: float32 [3072, 768], P('tensor', 'dp')
- grad_bias_query: float32 [768], P(('tensor', 'dp'))
- grad_bias_value: float32 [768], P(('tensor', 'dp'))
- grad_bias_out: float32 [768], P('dp')
- grad_bias_up: float32 [3072], P(('tensor', 'dp'))
- grad_bias_down: float32 [768], P('dp')
- grad_gain_attn: float32 [768], P('dp')
- grad_shift_attn: float32 [768], P('dp')
- grad_gain_out: float32 [768], P('dp')
- grad_shift_out: float32 [768], P('dp')
The draws below stay inside these ranges and needn't reach their ends.
Inputs may be any that keep to these rules, and one draw needn't show every extreme that they name: `segments`: within each sequence the numbers never fall; each document holds 1 to 768 tokens, one of them exactly 768.
All inputs are finite; a program needn't handle non-finite values.
Results may differ from the reference program's by a relative error of at most 0.025.
Values may be sent and summed in bfloat16 or wider, within the bound.
No kernel may reach another device: no remote copies, remote signals or barrier semaphores. Data moves between devices by JAX's collectives and lax.ppermute only.
A program may use at most 192 MiB of HBM per device.

```python
import math
import jax
import jax.numpy as jnp
import numpy as np
from jax import lax

D = 768
HEADS = 12
HEAD_DIM = 64
FF = 3072
SEQ_LEN = 1024
BLOCK = 64
WINDOW = 512
RAND = 3
DOCS = 4
NBLK = 16
NSEQ = 16
TOKENS = 16384
N_TENSOR = 4


def with_ends(array, rng, smallest, largest):
    index_at = [jax.random.randint(jax.random.fold_in(rng, axis), (), 0, length) for axis, length in enumerate(array.shape)]
    longest = array.shape.index(max(array.shape))
    next_to = index_at[:longest] + [(index_at[longest] + 1) % array.shape[longest]] + index_at[longest + 1:]
    return array.at[tuple(index_at)].set(smallest).at[tuple(next_to)].set(largest)


def spiked(values, rng, source, target, parts, factor):
    def block_of(axis_at):
        return (jnp.arange(values.shape[axis_at]) // (values.shape[axis_at] // parts)).reshape((-1,) + (1,) * (values.ndim - 1 - axis_at))

    one_side = jax.random.permutation(rng, parts)[block_of(target)]
    far = (block_of(target) + parts // 2) % parts
    return jnp.where((block_of(source) == one_side) | (block_of(source) == far), factor * values, values)


def shard_levels(key, dims, shards, low, largest):
    loudness = 1.0
    for axis_at, parts in shards:
        draws = jax.random.uniform(jax.random.fold_in(jax.random.fold_in(key, 6), axis_at), (parts,), jnp.float32, low / len(shards), largest / len(shards))
        loudness = loudness * jnp.repeat(jnp.exp(draws), dims[axis_at] // parts).reshape((-1,) + (1,) * (len(dims) - 1 - axis_at))
    return loudness


def split_up(number_of, total, reach, skew):
    loads = [(1 << 20) // math.isqrt(standing ** skew) + 1 for standing in range(2, number_of + 1)]
    rest, given = total - reach - (number_of - 1), [1] * (number_of - 1)
    while rest > 0:
        movable = [i for i in range(number_of - 1) if given[i] < reach]
        mass, left = sum([loads[i] for i in movable]), rest
        for i in movable:
            extra = min(reach - given[i], max(1, left * loads[i] // mass), rest)
            given[i] = given[i] + extra
            rest = rest - extra
    return np.array([reach] + given)


def uneven_parts(rng, count, total, reach, lean):
    if count == 2:
        one = jax.random.randint(rng, (), max(1, total - reach), min(reach, total - 1) + 1)
        return jnp.stack([one, total - one])
    sizes = jnp.asarray(split_up(count, total, reach, lean), jnp.int32)
    twos = (count - 1) // 2
    giver, receiver = sizes[1:1 + 2 * twos:2], sizes[2:2 + 2 * twos:2]
    slack = jnp.minimum(giver - 1, reach - receiver)
    passed = jax.random.randint(jax.random.fold_in(rng, 1), (twos,), 0, 1 << 20) % (slack + 1)
    sizes = sizes.at[1:1 + 2 * twos:2].set(giver - passed).at[2:2 + 2 * twos:2].set(receiver + passed)
    return sizes[jax.random.permutation(jax.random.fold_in(rng, 2), count)]


def bell_draw(own_key, shape, deviation, bound, split=(), held_as=jnp.bfloat16):
    drawn = deviation * jax.random.normal(own_key, shape, jnp.float32)
    if split:
        drawn = drawn * shard_levels(own_key, shape, split, -0.22, 0.18)
    return jnp.clip(drawn, -bound, bound).astype(held_as)


def bell_draw_with(rng, shape, deviation, most, cuts, heavy, held_as=jnp.bfloat16):
    values = deviation * jax.random.normal(rng, shape, jnp.float32)
    if cuts:
        values = values * shard_levels(rng, shape, cuts, -0.22, 0.18)
    return jnp.clip(spiked(values, jax.random.fold_in(rng, 3), *heavy), -most, most).astype(held_as)


def setup_inputs(seed: int = 0) -> dict:
    streams_of = jax.random.split(jax.random.key(seed), 20)
    tokens = bell_draw_with(streams_of[0], (TOKENS, D), 1.0, 6.0, ((0, 8),), (0, 1, 8, 2.0))
    segments = jax.vmap(lambda own: jnp.searchsorted(jnp.cumsum(uneven_parts(own, DOCS, SEQ_LEN, SEQ_LEN * 3 // 4, 2)), jnp.arange(SEQ_LEN), side="right"))(jax.random.split(streams_of[1], NSEQ)).reshape((NSEQ, SEQ_LEN)).astype(jnp.int32)
    random_blocks = with_ends(jax.random.randint(streams_of[2], (NBLK, HEADS, RAND), 0, SEQ_LEN // BLOCK), jax.random.fold_in(streams_of[2], 1), 0, (SEQ_LEN // BLOCK) - 1).astype(jnp.int32)
    w_query = bell_draw(streams_of[3], (D, D), D ** -0.5, 0.21875, ((0, 8), (1, 4)))
    w_key = bell_draw(streams_of[4], (D, D), D ** -0.5, 0.21875, ((0, 8), (1, 4)))
    w_value = bell_draw(streams_of[5], (D, D), D ** -0.5, 0.21875, ((0, 8), (1, 4)))
    w_out = bell_draw(streams_of[6], (D, D), (D // 16) ** -0.5, 0.875, ((0, 4), (1, 8)))
    w_up = bell_draw(streams_of[7], (D, FF), D ** -0.5, 0.21875, ((0, 8), (1, 4)))
    w_down = bell_draw(streams_of[8], (FF, D), FF ** -0.5, 0.109375, ((0, 4), (1, 8)))
    bias_query = bell_draw(streams_of[9], (D,), 0.3, 3.0, ((0, 32),))
    bias_value = bell_draw(streams_of[10], (D,), 0.5, 3.0, ((0, 32),))
    bias_out = bell_draw(streams_of[11], (D,), 0.5, 3.0, ((0, 8),))
    bias_up = bell_draw(streams_of[12], (FF,), 0.5, 3.0, ((0, 32),))
    bias_down = bell_draw(streams_of[13], (D,), 0.5, 3.0, ((0, 8),))
    gain_attn = jnp.clip(1.0 + 0.18 * jax.random.normal(streams_of[14], (D,), jnp.float32), 0.099609375, 1.8984375).astype(jnp.bfloat16)
    shift_attn = bell_draw(streams_of[15], (D,), 0.5, 3.0, ((0, 8),))
    gain_out = jnp.clip(1.0 + 0.18 * jax.random.normal(streams_of[16], (D,), jnp.float32), 0.099609375, 1.8984375).astype(jnp.bfloat16)
    shift_out = bell_draw(streams_of[17], (D,), 0.5, 3.0, ((0, 8),))
    cotangent = bell_draw_with(streams_of[18], (TOKENS, D), 1.0, 6.0, ((0, 8),), (0, 1, 8, 2.0))
    return {"tokens": tokens, "segments": segments, "random_blocks": random_blocks, "w_query": w_query, "w_key": w_key, "w_value": w_value, "w_out": w_out, "w_up": w_up, "w_down": w_down, "bias_query": bias_query, "bias_value": bias_value, "bias_out": bias_out, "bias_up": bias_up, "bias_down": bias_down, "gain_attn": gain_attn, "shift_attn": shift_attn, "gain_out": gain_out, "shift_out": shift_out, "cotangent": cotangent}


@jax.custom_vjp
def low(v):
    return lax.optimization_barrier(v.astype(jnp.bfloat16)).astype(jnp.float32)

@jax.custom_vjp
def low_back(v):
    return v

def low_keep(v):
    return (low(v), None)

def low_pass(kept, grad):
    return (grad,)

def back_keep(v):
    return (v, None)

def back_low(kept, grad):
    return (low(grad),)
low.defvjp(low_keep, low_pass)
low_back.defvjp(back_keep, back_low)

def norm_rows(values, gain_vec, shift_vec):
    center = values - lax.optimization_barrier(jnp.mean(values, axis=-1, keepdims=True))
    spread = lax.optimization_barrier(jnp.mean(center * center, axis=-1, keepdims=True))
    return center * lax.rsqrt(spread + 1e-12) * gain_vec + shift_vec

def gelu_tanh(values):
    return 0.5 * values * (1.0 + jnp.tanh(0.7978845608028654 * (values + 0.044715 * values * values * values)))

def allowed(random_blocks, segment_row):
    block_count = random_blocks.shape[0]
    length = segment_row.shape[0]
    block_len = length // block_count
    blocks = jnp.arange(block_count)
    near_blocks = jnp.abs(blocks[:, None] - blocks[None, :]) <= 1
    edge_blocks = (blocks == 0) | (blocks == block_count - 1)
    fixed_part = near_blocks | edge_blocks[None, :] | edge_blocks[:, None]
    picked = jnp.any(random_blocks[:, :, :, None] == blocks[None, None, None, :], axis=2)
    block_ok = fixed_part[None, :, :] | jnp.transpose(picked, (1, 0, 2))
    token_ok = jnp.repeat(jnp.repeat(block_ok, block_len, axis=1), block_len, axis=2)
    places = jnp.arange(length)
    inside = jnp.abs(places[:, None] - places[None, :]) < WINDOW
    same_doc = segment_row[:, None] == segment_row[None, :]
    return token_ok & (inside & same_doc)[None, :, :]

def product(left, right):
    return jnp.dot(left, right, precision=lax.Precision.HIGHEST)

def sequence_layer(params, tok_row, segment_row, random_blocks):
    w_query, w_key, w_value, w_out, w_up, w_down, bias_query, bias_value, bias_out, bias_up, bias_down, gain_attn, shift_attn, gain_out, shift_out = params
    length = tok_row.shape[0]
    width_dev = D // N_TENSOR
    heads_dev = HEADS // N_TENSOR
    hidden_dev = FF // N_TENSOR
    score_scale = HEAD_DIM ** (-0.5)
    allowed_all = allowed(random_blocks, segment_row)
    tok_low = low(tok_row)
    attn_sum = jnp.zeros_like(tok_row)
    for group_index in range(N_TENSOR):
        col_start = group_index * width_dev
        col_stop = col_start + width_dev
        tok_group = low_back(tok_low)
        query = low(low_back(product(tok_group, w_query[:, col_start:col_stop]) + bias_query[col_start:col_stop]))
        key_rows = low(low_back(product(tok_group, w_key[:, col_start:col_stop])))
        value_rows = low(low_back(product(tok_group, w_value[:, col_start:col_stop]) + bias_value[col_start:col_stop]))
        query = query.reshape(length, heads_dev, HEAD_DIM)
        key_rows = key_rows.reshape(length, heads_dev, HEAD_DIM)
        value_rows = value_rows.reshape(length, heads_dev, HEAD_DIM)
        scores = low_back(jnp.einsum('qhd,khd->hqk', query, key_rows, precision=lax.Precision.HIGHEST) * score_scale)
        scores = jnp.where(allowed_all[group_index * heads_dev:(group_index + 1) * heads_dev], scores, -1e+30)
        row_max = lax.optimization_barrier(jnp.max(scores, axis=-1, keepdims=True))
        exp_scores = jnp.exp(scores - row_max)
        prob_full = exp_scores / lax.optimization_barrier(jnp.sum(exp_scores, axis=-1, keepdims=True))
        context = jnp.einsum('hqk,khd->qhd', low(prob_full), value_rows, precision=lax.Precision.HIGHEST)
        context = low(low_back(context.reshape(length, width_dev)))
        attn_sum = attn_sum + low(low_back(product(context, w_out[col_start:col_stop, :])))
    hidden_in = tok_row + attn_sum + bias_out
    normed = norm_rows(hidden_in, gain_attn, shift_attn)
    normed_low = low(normed)
    mlp_sum = jnp.zeros_like(normed)
    for group_index in range(N_TENSOR):
        ff_start = group_index * hidden_dev
        ff_stop = ff_start + hidden_dev
        normed_group = low_back(normed_low)
        up_proj = low_back(product(normed_group, w_up[:, ff_start:ff_stop]) + bias_up[ff_start:ff_stop])
        act_low = low(gelu_tanh(up_proj))
        mlp_sum = mlp_sum + low(low_back(product(act_low, w_down[ff_start:ff_stop, :])))
    summed = normed + mlp_sum + bias_down
    return norm_rows(summed, gain_out, shift_out)

def widen(matrix):
    return matrix.astype(jnp.float32)

def reference(tokens, segments, random_blocks, w_query, w_key, w_value, w_out, w_up, w_down, bias_query, bias_value, bias_out, bias_up, bias_down, gain_attn, shift_attn, gain_out, shift_out, cotangent):
    params = (widen(w_query), widen(w_key), widen(w_value), widen(w_out), widen(w_up), widen(w_down), widen(bias_query), widen(bias_value), widen(bias_out), widen(bias_up), widen(bias_down), widen(gain_attn), widen(shift_attn), widen(gain_out), widen(shift_out))
    tok_input = tokens.astype(jnp.float32)

    def forward(params_in, tok_all):
        layer_fn = jax.checkpoint(sequence_layer)

        def one_sequence(carried, seq_items):
            tok_row, segment_row = seq_items
            return (carried, layer_fn(params_in, tok_row, segment_row, random_blocks))
        _, result = lax.scan(one_sequence, jnp.zeros((), jnp.float32), (tok_all.reshape(-1, SEQ_LEN, D), segments))
        return result.reshape(-1, D)
    output, pullback = jax.vjp(forward, params, tok_input)
    grad_params, grad_input = pullback(cotangent.astype(jnp.float32))
    return (output.astype(jnp.bfloat16), grad_input, grad_params[0], grad_params[1], grad_params[2], grad_params[3], grad_params[4], grad_params[5], grad_params[6], grad_params[7], grad_params[8], grad_params[9], grad_params[10], grad_params[11], grad_params[12], grad_params[13], grad_params[14])
```

```python
import functools

import jax
import jax.numpy as jnp
from jax import lax
from jax.experimental import pallas as pl
from jax.experimental.pallas import tpu as pltpu
from jax.sharding import PartitionSpec as P

BIG = -1e30
NN = (((1,), (0,)), ((), ()))
NT = (((1,), (1,)), ((), ()))
TN = (((0,), (0,)), ((), ()))
f32 = jnp.float32
bf16 = jnp.bfloat16
D = 768
SLOT = 256
VEC = 16
VMEM = pl.BlockSpec(memory_space=pltpu.VMEM)
SMEM = pl.BlockSpec(memory_space=pltpu.SMEM)


def sds(shape, dtype):
    return jax.ShapeDtypeStruct(shape, dtype)


def cost(flops, nbytes):
    return pl.CostEstimate(flops=int(flops), bytes_accessed=int(nbytes), transcendentals=0)


def dot(a,b,dn=NN): return lax.dot_general(a,b,dn,preferred_element_type=f32)

def aug_kernel(sc_ref, seg_ref, rb_ref, rbo_ref, qaug_ref, kaug_ref):
    hi=sc_ref[9]
    length=seg_ref.shape[1]; nblk=16; bl=length//nblk
    seg=seg_ref[pl.ds(hi,1),:]
    row=lax.broadcasted_iota(jnp.int32,(128,length),0)
    tok=lax.broadcasted_iota(jnp.int32,(128,length),1)
    blk=tok//bl
    qa=jnp.where((row>=64)&(row<80)&(blk==row-64),1.0,0.0)+jnp.where((row>=80)&(row<84)&(seg==row-80),1.0,0.0)
    qaug_ref[...]=jnp.transpose(qa.astype(f32)).astype(bf16)
    r16=lax.broadcasted_iota(jnp.int32,(16,length),0)
    b16=lax.broadcasted_iota(jnp.int32,(16,length),1)//bl
    near=jnp.abs(r16-b16)<=1
    edge=(r16==0)|(r16==nblk-1)|(b16==0)|(b16==nblk-1)
    inwin=jnp.abs(r16-b16)<=8
    r48=lax.broadcasted_iota(jnp.int32,(48,length),0)
    segb=jnp.where((r48<4)&(seg!=r48),BIG,0.0)
    z64=jnp.zeros((64,length),f32)
    for g,ref in ((0,rb_ref),(1,rbo_ref)):
        for h in range(3):
            ok=near|edge
            for r in range(3):
                ok=ok|(ref[:,h*3+r:h*3+r+1]==b16)
            bb=jnp.where(ok&inwin,0.0,BIG)
            kaug_ref[g*3+h]=jnp.transpose(jnp.concatenate([z64,bb,segb],axis=0)).astype(bf16)

def head_keys(k, kaug, h):
    lane=lax.broadcasted_iota(jnp.int32,k.shape,1)
    kh=jnp.where(lane//64==h,k,jnp.zeros_like(k))
    return jnp.concatenate([kh[:,:128],kh[:,128:]+kaug],axis=1)

def attn_fwd_kernel(qkv_ref, kaug_ref, ctx_ref, lse_ref):
    h=pl.program_id(0)
    length=qkv_ref.shape[0]
    k=qkv_ref[:,256:512]; v=qkv_ref[:,512:768]
    lane=lax.broadcasted_iota(jnp.int32,k.shape,1)
    kh=head_keys(k,kaug_ref[0],h)
    vh=jnp.where(lane//64==h,v,jnp.where(lane==192,1.0,0.0).astype(bf16))
    tq=256
    for t in range(length//tq):
        lo=max(0,t-2)*tq; up=min(length//tq,t+3)*tq
        s=dot(qkv_ref[t*tq:(t+1)*tq,0:256],kh[lo:up],NT)
        if True:
            parts=[]
            for u in range(lo//tq,up//tq):
                c=s[:,(u*tq-lo):(u*tq-lo)+tq]
                if abs(u-t)==2:
                    ii=lax.broadcasted_iota(jnp.int32,c.shape,0); jj=lax.broadcasted_iota(jnp.int32,c.shape,1)
                    c=jnp.where((jj-ii>0) if u<t else (ii-jj>0),c,BIG)
                parts.append(c)
            s=jnp.concatenate(parts,axis=1)
        m=jnp.max(s,axis=1,keepdims=True)
        p=jnp.exp(s-m).astype(bf16)
        o=dot(p,vh[lo:up])
        l=o[:,192:193]
        lse=m+jnp.log(l)
        o=(o/l).astype(bf16)
        lse_ref[0,:,t*tq:(t+1)*tq]=jnp.transpose(jnp.broadcast_to(lse,(tq,128)))[0:8,:]
        ol=lax.broadcasted_iota(jnp.int32,o.shape,1)
        keep=jnp.where(h==0,jnp.zeros_like(o),ctx_ref[t*tq:(t+1)*tq,:])
        ctx_ref[t*tq:(t+1)*tq,:]=jnp.where(ol//64==h,o,keep)

def attn_fwd(qkv,kaug,g):
    L=qkv.shape[0]
    return pl.pallas_call(attn_fwd_kernel,grid=(3,),
        in_specs=[pl.BlockSpec((L,768),lambda h:(0,0)),pl.BlockSpec((1,L,128),lambda h:(g*3+h,0,0))],
        out_specs=[pl.BlockSpec((L,256),lambda h:(0,0)),pl.BlockSpec((1,8,L),lambda h:(h,0,0))],
        out_shape=[jax.ShapeDtypeStruct((L,256),bf16),jax.ShapeDtypeStruct((3,8,L),f32)],name="attn_fwd")(qkv,kaug)

def attn_bwd_kernel(qkv_ref,kaug_ref,ctx_ref,lse_ref,do_ref,out_ref,dk_acc,dv_acc,dq_acc):
    h=pl.program_id(0)
    length=qkv_ref.shape[0]
    k=qkv_ref[:,256:512]; v=qkv_ref[:,512:768]
    lane=lax.broadcasted_iota(jnp.int32,k.shape,1)
    mh=lane//64==h
    kh=head_keys(k,kaug_ref[0],h)
    zero=jnp.zeros_like(k)
    vh=jnp.where(mh,v,zero)
    doh=jnp.where(mh,do_ref[...],zero)
    qh=jnp.where(mh,qkv_ref[:,0:256],zero)
    @pl.when(h==0)
    def _():
        dk_acc[...]=jnp.zeros_like(dk_acc); dv_acc[...]=jnp.zeros_like(dv_acc); dq_acc[...]=jnp.zeros_like(dq_acc)
    prod=doh.astype(f32)*ctx_ref[...].astype(f32)
    hi=prod.astype(bf16); lo_=(prod-hi.astype(f32)).astype(bf16)
    ones=jnp.ones((8,256),bf16)
    drow=dot(ones,hi,NT)+dot(ones,lo_,NT)
    tq=256
    for t in range(length//tq):
        lo=max(0,t-2)*tq; up=min(length//tq,t+3)*tq
        qs=slice(t*tq,(t+1)*tq)
        st=dot(kh[lo:up],qkv_ref[qs,0:256],NT)
        parts=[]
        for u in range(lo//tq,up//tq):
            c=st[(u*tq-lo):(u*tq-lo)+tq]
            if abs(u-t)==2:
                jj=lax.broadcasted_iota(jnp.int32,c.shape,0); ii=lax.broadcasted_iota(jnp.int32,c.shape,1)
                c=jnp.where((jj-ii>0) if u<t else (ii-jj>0),c,BIG)
            parts.append(c)
        st=jnp.concatenate(parts,axis=0)
        pt=jnp.exp(st-lse_ref[0,0:1,qs])
        dpt=dot(vh[lo:up],do_ref[qs,:],NT)
        dv_acc[lo:up,:]+=dot(pt.astype(bf16),doh[qs,:])
        ds=(pt*(dpt-drow[0:1,qs])).astype(bf16)
        dk_acc[lo:up,:]+=dot(ds,qh[qs,:])
        dq_acc[qs,:]+=dot(ds,kh[lo:up],TN)
    @pl.when(h==2)
    def _():
        keep=lane<192
        out_ref[:,0:256]=jnp.where(keep,dq_acc[...]*0.125,0.0).astype(bf16)
        out_ref[:,256:512]=dk_acc[...].astype(bf16)
        out_ref[:,512:768]=dv_acc[...].astype(bf16)

def attn_bwd(qkv,kaug,ctx,lse,do,g):
    L=qkv.shape[0]
    full=lambda h:(0,0)
    return pl.pallas_call(attn_bwd_kernel,grid=(3,),
        in_specs=[pl.BlockSpec((L,768),full),pl.BlockSpec((1,L,128),lambda h:(g*3+h,0,0)),pl.BlockSpec((L,256),full),
                  pl.BlockSpec((1,8,L),lambda h:(h,0,0)),pl.BlockSpec((L,256),full)],
        out_specs=pl.BlockSpec((L,768),full),
        out_shape=jax.ShapeDtypeStruct((L,768),bf16),
        scratch_shapes=[pltpu.VMEM((L,256),f32)]*3,name="attn_bwd")(qkv,kaug,ctx,lse,do)

def prep(sc,seg,rb,rbo):
    L=seg.shape[1]
    return pl.pallas_call(aug_kernel,grid_spec=pltpu.PrefetchScalarGridSpec(num_scalar_prefetch=1,grid=(1,),
        in_specs=[pl.BlockSpec(seg.shape,lambda i,s:(0,0)),pl.BlockSpec((16,9),lambda i,s:(0,0)),pl.BlockSpec((16,9),lambda i,s:(0,0))],
        out_specs=[pl.BlockSpec((L,128),lambda i,s:(0,0)),pl.BlockSpec((6,L,128),lambda i,s:(0,0,0))]),
        out_shape=[jax.ShapeDtypeStruct((L,128),bf16),jax.ShapeDtypeStruct((6,L,128),bf16)],name="aug")(sc,seg,rb,rbo)


class Blocks:
    def __init__(self, count, rows, stride):
        self.count, self.rows, self.stride = count, rows, stride


def copy_blocks(blocks, refs, table, put):
    per = blocks.count // len(refs)
    for b in range(blocks.count):
        ref = refs[b // per]
        base = (b % per) * blocks.stride
        if blocks.count == 1:
            put(0, ref, base, blocks.rows)
        else:
            put(pl.multiple_of(table[b] * blocks.rows, 16), ref, base, blocks.rows)


def pack_first_kernel(wq, wk, wv, bq, bv, bup, bout, bdown, ga, sa, go, so, out):
    rows = wq.shape[0]
    out[0:rows, 0:192] = wq[...]
    out[0:rows, 192:384] = wk[...]
    out[0:rows, 384:576] = wv[...]
    out[rows : rows + VEC, :] = jnp.zeros((VEC, 576), bf16)
    lines = []
    for vec in (bq, bv, bup, bout, bdown, ga, sa, go, so):
        size = vec.shape[0]
        line = vec[...].astype(f32).reshape(1, size)
        lines.append(jnp.concatenate([line, jnp.zeros((1, 128 - size), f32)], axis=1))
    lines.append(jnp.zeros((VEC - 9, 128), f32))
    out[rows : rows + VEC, 0:128] = jnp.concatenate(lines, axis=0).astype(bf16)


def pack_rest_kernel(wo, wu, wd, second, third):
    second[:, 0:192] = jnp.transpose(wo[...].astype(f32)).astype(bf16)
    second[:, 192:960] = wu[...]
    third[...] = jnp.transpose(wd[...].astype(f32)).astype(bf16)


def unpack_vectors(blocks, refs, table):
    per = blocks.count // len(refs)
    row = lax.broadcasted_iota(jnp.int32, (128, D), 0)
    col = lax.broadcasted_iota(jnp.int32, (128, D), 1)
    wide = jnp.where((row < 96) & (col % 96 == row), 1.0, 0.0).astype(bf16)
    thin = jnp.where((row < 24) & (col % 24 == row) & (col < 192), 1.0, 0.0).astype(bf16)
    col1 = lax.broadcasted_iota(jnp.int32, (VEC, D), 1)
    line = lax.broadcasted_iota(jnp.int32, (VEC, D), 0)
    total = jnp.zeros((VEC, D), f32)
    for b in range(blocks.count):
        base = (b % per) * blocks.stride + blocks.rows
        part = refs[b // per][base : base + VEC, 0:128]
        ours = jnp.where(line < 2, col1 // 24, col1 // 96) == table[b]
        spread = jnp.where(line < 2, dot(part, thin), dot(part, wide))
        total = total + jnp.where(ours, spread, 0.0)
    return total


def project_kernel(blocks, sc, tok, qaug, *refs):
    ins, (qkv, vec, weight) = refs[:-3], refs[-3:]

    @pl.when(pl.program_id(0) == 0)
    def _():
        weight[...] = jnp.zeros_like(weight)

        def put(at, ref, base, rows):
            for part in range(3):
                weight[pl.ds(at, rows), part * 256 : part * 256 + 192] = ref[
                    base : base + rows, part * 192 : part * 192 + 192
                ]

        copy_blocks(blocks, ins[: len(ins) - (blocks.count == 1)], sc, put)
        if blocks.count == 1:
            vec[...] = ins[-1][...]
        else:
            vec[...] = unpack_vectors(blocks, ins, sc)

    y = dot(tok[...], weight[...])
    query = (y[:, 0:256] + vec[0:1, 0:256]).astype(bf16) * jnp.asarray(0.125, bf16)
    qkv[:, 0:128] = query[:, 0:128]
    qkv[:, 128:256] = query[:, 128:256] + qaug[...]
    qkv[:, 256:512] = y[:, 256:512].astype(bf16)
    qkv[:, 512:768] = (y[:, 512:768] + vec[1:2, 0:256]).astype(bf16)


def project(blocks, sc, tokens, qaug, group):
    length = qaug.shape[0]
    tile = 256
    steps = length // tile
    ins = list(group)
    return pl.pallas_call(
        functools.partial(project_kernel, blocks),
        grid_spec=pltpu.PrefetchScalarGridSpec(
            num_scalar_prefetch=1,
            grid=(steps,),
            in_specs=[
                pl.BlockSpec((tile, D), lambda i, s: (s[9] * steps + i, 0)),
                pl.BlockSpec((tile, 128), lambda i, s: (i, 0)),
            ]
            + [pl.BlockSpec(a.shape, lambda i, s: (0, 0)) for a in ins],
            out_specs=[
                pl.BlockSpec((tile, 768), lambda i, s: (i, 0)),
                pl.BlockSpec((VEC, D), lambda i, s: (0, 0)),
            ],
            scratch_shapes=[pltpu.VMEM((D, 768), bf16)],
        ),
        out_shape=[sds((length, 768), bf16), sds((VEC, D), f32)],
        cost_estimate=cost(2 * length * D * 768, 5e6),
        name="project",
    )(sc, tokens, qaug, *ins)


def load_out(blocks, sc, refs, scratch):
    scratch[...] = jnp.zeros_like(scratch)

    def put(at, ref, base, rows):
        scratch[pl.ds(at, rows), 0:192] = ref[base : base + rows, 0:192]

    copy_blocks(blocks, refs, sc, put)


def load_up(blocks, sc, refs, scratch):
    def put(at, ref, base, rows):
        scratch[pl.ds(at, rows), :] = ref[base : base + rows, 192:960]

    copy_blocks(blocks, refs, sc, put)


def load_down(blocks, sc, refs, scratch):
    def put(at, ref, base, rows):
        scratch[pl.ds(at, rows), :] = ref[base : base + rows, :]

    copy_blocks(blocks, refs, sc, put)


def load_qkv(blocks, sc, refs, scratch):
    scratch[...] = jnp.zeros_like(scratch)

    def put(at, ref, base, rows):
        for part in range(3):
            scratch[pl.ds(at, rows), part * 256 : part * 256 + 192] = ref[
                base : base + rows, part * 192 : part * 192 + 192
            ]

    copy_blocks(blocks, refs, sc, put)


def out_project_kernel(blocks, count, sc, ctx_a, ctx_b, *refs):
    ins, (give, keep, wa, wb) = refs[: 2 * count], refs[2 * count :]
    half = give.shape[0]
    load_out(blocks, sc, ins[:count], wa)
    load_out(blocks, sc, ins[count:], wb)
    core = sc[8]

    def part(which):
        rows = pl.ds(pl.multiple_of(which * half, half), half)
        return dot(ctx_a[rows, :], wa[...], NT) + dot(ctx_b[rows, :], wb[...], NT)

    give[...] = part(1 - core).astype(bf16)
    keep[...] = part(core)


def whole(kernel, ins, outs, scratch=(), flops=1e9, name=None):
    nbytes = sum(a.size * a.dtype.itemsize for a in ins) + sum(
        a.size * jnp.dtype(a.dtype).itemsize for a in outs
    )
    return pl.pallas_call(
        kernel,
        in_specs=[SMEM] + [VMEM] * (len(ins) - 1),
        out_specs=[VMEM] * len(outs),
        out_shape=outs,
        scratch_shapes=list(scratch),
        cost_estimate=cost(flops, nbytes),
        name=name,
    )(*ins)


def normalize(v):
    center = v - jnp.mean(v, axis=-1, keepdims=True)
    spread = jnp.mean(center * center, axis=-1, keepdims=True)
    inv = lax.rsqrt(spread + 1e-12)
    return center * inv, inv


def normalize_back(n, inv, dn):
    return inv * (
        dn - jnp.mean(dn, axis=-1, keepdims=True) - n * jnp.mean(dn * n, axis=-1, keepdims=True)
    )


def norm_one_kernel(sc, keep, got, tok, vec, normal, low, inv_out):
    v = tok[...].astype(f32) + (keep[...] + got[...].astype(f32)) + vec[3:4, :]
    n, inv = normalize(v)
    normal[...] = n
    inv_out[...] = jnp.broadcast_to(inv, inv_out.shape)
    low[...] = (n * vec[5:6, :] + vec[6:7, :]).astype(bf16)


def norm_one(sc, keep, got, tokens, vec):
    half = keep.shape[0]
    tile = 256
    steps = half // tile
    row = lambda i, s: (i, 0)
    return pl.pallas_call(
        norm_one_kernel,
        grid_spec=pltpu.PrefetchScalarGridSpec(
            num_scalar_prefetch=1,
            grid=(steps,),
            in_specs=[
                pl.BlockSpec((tile, D), row),
                pl.BlockSpec((tile, D), row),
                pl.BlockSpec((tile, D), lambda i, s: ((s[9] * 2 + s[8]) * steps + i, 0)),
                pl.BlockSpec((VEC, D), lambda i, s: (0, 0)),
            ],
            out_specs=[
                pl.BlockSpec((tile, D), row),
                pl.BlockSpec((tile, D), row),
                pl.BlockSpec((tile, 128), row),
            ],
        ),
        out_shape=[sds((half, D), f32), sds((half, D), bf16), sds((half, 128), f32)],
        cost_estimate=cost(1e7, 8e6),
        name="norm_one",
    )(sc, keep, got, tokens, vec)


def mlp_kernel(blocks, count, sc, x, vec_a, vec_b, *refs):
    ins, (act_a, act_b, slope_a, slope_b, part, wu, wd_a, wd_b) = refs[: 4 * count], refs[4 * count :]
    step = pl.program_id(0)

    @pl.when(step == 0)
    def _():
        load_up(blocks, sc, ins[:count], wu.at[0])
        load_up(blocks, sc, ins[count : 2 * count], wu.at[1])
        load_down(blocks, sc, ins[2 * count : 3 * count], wd_a)
        load_down(blocks, sc, ins[3 * count :], wd_b)

    total = None
    for g, (vec, act_ref, slope_ref, wd) in enumerate(
        ((vec_a, act_a, slope_a, wd_a), (vec_b, act_b, slope_b, wd_b))
    ):
        u = dot(x[...], wu[g]) + vec[2:3, :]
        square = u * u
        t = jnp.tanh(0.7978845608028654 * (u + 0.044715 * square * u))
        act = (0.5 * u * (1.0 + t)).astype(bf16)
        slope = 0.5 * (1.0 + t) + (0.5 * 0.7978845608028654) * u * (1.0 - t * t) * (
            1.0 + (3 * 0.044715) * square
        )
        act_ref[...] = act
        slope_ref[...] = slope.astype(bf16)
        y = dot(act, wd[...], NT)
        total = y if total is None else total + y
    part[...] = total.astype(part.dtype)


def mlp(blocks, sc, x, vec_a, vec_b, ups, downs, out_dtype):
    half = x.shape[0]
    tile = 256
    ins = list(ups[0]) + list(ups[1]) + list(downs[0]) + list(downs[1])
    count = len(ups[0])
    row = lambda i, s: (i, 0)
    zero = lambda i, s: (0, 0)
    return pl.pallas_call(
        functools.partial(mlp_kernel, blocks, count),
        grid_spec=pltpu.PrefetchScalarGridSpec(
            num_scalar_prefetch=1,
            grid=(half // tile,),
            in_specs=[
                pl.BlockSpec((tile, D), row),
                pl.BlockSpec((VEC, D), zero),
                pl.BlockSpec((VEC, D), zero),
            ]
            + [pl.BlockSpec(a.shape, zero) for a in ins],
            out_specs=[pl.BlockSpec((tile, D), row)] * 5,
            scratch_shapes=[pltpu.VMEM((2, D, D), bf16), pltpu.VMEM((D, D), bf16), pltpu.VMEM((D, D), bf16)],
        ),
        out_shape=[sds((half, D), bf16)] * 4 + [sds((half, D), out_dtype)],
        cost_estimate=cost(8 * half * D * D, 1.2e7),
        name="mlp",
    )(sc, x, vec_a, vec_b, *ins)


def norm_two_kernel(sc, keep, got, normal, vec, cot, out, d_low, d_sum, sums):
    step = pl.program_id(0)
    normed = normal[...] * vec[5:6, :] + vec[6:7, :]
    v = normed + (keep[...] + got[...].astype(f32)) + vec[4:5, :]
    n, inv = normalize(v)
    out[...] = (n * vec[7:8, :] + vec[8:9, :]).astype(bf16)
    dy = cot[...].astype(f32)
    d = normalize_back(n, inv, dy * vec[7:8, :])
    d_sum[...] = d
    d_low[...] = d.astype(bf16)

    @pl.when(step == 0)
    def _():
        sums[...] = jnp.zeros_like(sums)

    sums[0:1, :] += jnp.sum(d, axis=0, keepdims=True)
    sums[1:2, :] += jnp.sum(dy * n, axis=0, keepdims=True)
    sums[2:3, :] += jnp.sum(dy, axis=0, keepdims=True)


def norm_two(sc, keep, got, normal, vec, cotangent):
    half = keep.shape[0]
    tile = 256
    steps = half // tile
    row = lambda i, s: (i, 0)
    own = lambda i, s: ((s[9] * 2 + s[8]) * steps + i, 0)
    return pl.pallas_call(
        norm_two_kernel,
        grid_spec=pltpu.PrefetchScalarGridSpec(
            num_scalar_prefetch=1,
            grid=(steps,),
            in_specs=[pl.BlockSpec((tile, D), row)] * 3
            + [pl.BlockSpec((VEC, D), lambda i, s: (0, 0)), pl.BlockSpec((tile, D), own)],
            out_specs=[pl.BlockSpec((tile, D), row)] * 3 + [pl.BlockSpec((8, D), lambda i, s: (0, 0))],
        ),
        out_shape=[sds((half, D), bf16), sds((half, D), bf16), sds((half, D), f32), sds((8, D), f32)],
        cost_estimate=cost(2e7, 1e7),
        name="norm_two",
    )(sc, keep, got, normal, vec, cotangent)


def mlp_back_kernel(blocks, count, sc, d, slope_a, slope_b, *refs):
    ins, (up_a, up_b, part, sums, wu, wd) = refs[: 4 * count], refs[4 * count :]
    step = pl.program_id(0)

    @pl.when(step == 0)
    def _():
        load_up(blocks, sc, ins[:count], wu.at[0])
        load_up(blocks, sc, ins[count : 2 * count], wu.at[1])
        load_down(blocks, sc, ins[2 * count : 3 * count], wd.at[0])
        load_down(blocks, sc, ins[3 * count :], wd.at[1])
        sums[...] = jnp.zeros_like(sums)

    total = None
    for g, (slope, up) in enumerate(((slope_a, up_a), (slope_b, up_b))):
        du = dot(d[...], wd[g]) * slope[...].astype(f32)
        low = du.astype(bf16)
        up[...] = low
        sums[g : g + 1, :] += jnp.sum(du, axis=0, keepdims=True)
        y = dot(low, wu[g], NT)
        total = y if total is None else total + y
    part[...] = total.astype(part.dtype)


def mlp_back(blocks, sc, d, slopes, ups, downs, out_dtype):
    half = d.shape[0]
    tile = 256
    ins = list(ups[0]) + list(ups[1]) + list(downs[0]) + list(downs[1])
    count = len(ups[0])
    row = lambda i, s: (i, 0)
    zero = lambda i, s: (0, 0)
    return pl.pallas_call(
        functools.partial(mlp_back_kernel, blocks, count),
        grid_spec=pltpu.PrefetchScalarGridSpec(
            num_scalar_prefetch=1,
            grid=(half // tile,),
            in_specs=[pl.BlockSpec((tile, D), row)] * 3 + [pl.BlockSpec(a.shape, zero) for a in ins],
            out_specs=[pl.BlockSpec((tile, D), row)] * 3 + [pl.BlockSpec((8, D), zero)],
            scratch_shapes=[pltpu.VMEM((2, D, D), bf16), pltpu.VMEM((2, D, D), bf16)],
        ),
        out_shape=[sds((half, D), bf16)] * 2 + [sds((half, D), out_dtype), sds((8, D), f32)],
        cost_estimate=cost(8 * half * D * D, 1.2e7),
        name="mlp_back",
    )(sc, d, slopes[0], slopes[1], *ins)


def put_blocks(blocks, table, acc, out, lo, width, col):
    for b in range(blocks.count):
        at = 0 if blocks.count == 1 else pl.multiple_of(table[b] * blocks.rows, 16)
        out[b * blocks.stride : b * blocks.stride + blocks.rows, col : col + width] = acc[
            pl.ds(at, blocks.rows), lo : lo + width
        ].astype(bf16)


def grad_down_kernel(blocks, sc, d_own, d_oth, aa_own, aa_oth, ab_own, ab_oth, ga, gb, acc):
    for own, oth, out in ((aa_own, aa_oth, ga), (ab_own, ab_oth, gb)):
        acc[...] = dot(d_own[...], own[...], TN) + dot(d_oth[...], oth[...], TN)
        put_blocks(blocks, sc, acc, out, 0, D, 0)


def grad_up_kernel(blocks, sc, n_own, n_oth, ua_own, ua_oth, ub_own, ub_oth, dc, ctx_a, ctx_b, ga, gb, acc):
    for own, oth, ctx, out in ((ua_own, ua_oth, ctx_a, ga), (ub_own, ub_oth, ctx_b, gb)):
        acc[...] = dot(n_own[...], own[...], TN) + dot(n_oth[...], oth[...], TN)
        put_blocks(blocks, sc, acc, out, 0, D, 192)
        acc[:, 0:256] = dot(dc[...], ctx[...], TN)
        put_blocks(blocks, sc, acc, out, 0, 192, 0)


def norm_one_back_kernel(sc, keep, got, d_sum, normal, inv, vec, d_hid, d_low, sums):
    step = pl.program_id(0)
    dy = d_sum[...] + (keep[...] + got[...].astype(f32))
    n = normal[...]
    d = normalize_back(n, inv[:, 0:1], dy * vec[5:6, :])
    d_hid[...] = d
    d_low[...] = d.astype(bf16)

    @pl.when(step == 0)
    def _():
        sums[...] = jnp.zeros_like(sums)

    sums[0:1, :] += jnp.sum(d, axis=0, keepdims=True)
    sums[1:2, :] += jnp.sum(dy * n, axis=0, keepdims=True)
    sums[2:3, :] += jnp.sum(dy, axis=0, keepdims=True)


def norm_one_back(sc, keep, got, d_sum, normal, inv, vec):
    half = keep.shape[0]
    tile = 256
    row = lambda i, s: (i, 0)
    zero = lambda i, s: (0, 0)
    return pl.pallas_call(
        norm_one_back_kernel,
        grid_spec=pltpu.PrefetchScalarGridSpec(
            num_scalar_prefetch=1,
            grid=(half // tile,),
            in_specs=[pl.BlockSpec((tile, D), row)] * 4
            + [pl.BlockSpec((tile, 128), row), pl.BlockSpec((VEC, D), zero)],
            out_specs=[pl.BlockSpec((tile, D), row)] * 2 + [pl.BlockSpec((8, D), zero)],
        ),
        out_shape=[sds((half, D), f32), sds((half, D), bf16), sds((8, D), f32)],
        cost_estimate=cost(2e7, 1e7),
        name="norm_one_back",
    )(sc, keep, got, d_sum, normal, inv, vec)


def d_context_kernel(blocks, count, sc, d_own, d_oth, *refs):
    ins, (d_all, da, db, wa) = refs[: 2 * count], refs[2 * count :]
    half = d_own.shape[0]
    core = sc[8]
    d_all[pl.ds(pl.multiple_of(core * half, half), half), :] = d_own[...]
    d_all[pl.ds(pl.multiple_of((1 - core) * half, half), half), :] = d_oth[...]
    for part, out in ((ins[:count], da), (ins[count:], db)):
        load_out(blocks, sc, part, wa)
        out[...] = dot(d_all[...], wa[...]).astype(bf16)


def grad_qkv_kernel(blocks, sc, tok, dqkv, sums_up, sums_rep, out, vec_out, acc):
    length = dqkv.shape[0]
    x = tok[pl.ds(pl.multiple_of(sc[9] * length, length), length), :]
    acc[...] = dot(x, dqkv[...], TN)
    for part in range(3):
        put_blocks(blocks, sc, acc, out, part * 256, 192, part * 192)
    total = jnp.sum(dqkv[...].astype(f32), axis=0, keepdims=True)
    pad = jnp.zeros((1, D - 256), f32)
    lines = jnp.concatenate(
        [
            jnp.concatenate([total[:, 0:256], pad], axis=1),
            jnp.concatenate([total[:, 512:768], pad], axis=1),
            sums_up[...],
            sums_rep[0:6, :],
            jnp.zeros((VEC - 9, D), f32),
        ],
        axis=0,
    )
    vec_out[...] = lines
    if blocks.count > 1:
        line = lax.broadcasted_iota(jnp.int32, (VEC, D), 0)
        col = lax.broadcasted_iota(jnp.int32, (VEC, D), 1)
        row_t = lax.broadcasted_iota(jnp.int32, (D, 128), 0)
        col_t = lax.broadcasted_iota(jnp.int32, (D, 128), 1)
        wide = jnp.where((col_t < 96) & (row_t % 96 == col_t), 1.0, 0.0).astype(bf16)
        thin = jnp.where((col_t < 24) & (row_t % 24 == col_t) & (row_t < 192), 1.0, 0.0).astype(bf16)
        where = jnp.where(line < 2, col // 24, col // 96)
        low = lines.astype(bf16)
        line_t = lax.broadcasted_iota(jnp.int32, (VEC, 128), 0)
        for b in range(blocks.count):
            part = jnp.where(where == sc[b], low, jnp.zeros_like(low))
            piece = jnp.where(line_t < 2, dot(part, thin), dot(part, wide)).astype(bf16)
            base = b * blocks.stride + blocks.rows
            out[base : base + VEC, 0:128] = piece
            out[base : base + VEC, 128:576] = jnp.zeros((VEC, 448), bf16)


def d_input_kernel(blocks, count, sc, da, db, *refs):
    ins, (give, keep, wa, wb) = refs[: 2 * count], refs[2 * count :]
    half = give.shape[0]
    load_qkv(blocks, sc, ins[:count], wa)
    load_qkv(blocks, sc, ins[count:], wb)
    core = sc[8]

    def part(which):
        rows = pl.ds(pl.multiple_of(which * half, half), half)
        return dot(da[rows, :], wa[...], NT) + dot(db[rows, :], wb[...], NT)

    give[...] = part(1 - core).astype(bf16)
    keep[...] = part(core)


def final_first_kernel(rows, p0, p1, p2, p3, gq, gk, gv, *vecs):
    total = p0[...].astype(f32) + p1[...].astype(f32) + p2[...].astype(f32) + p3[...].astype(f32)
    gq[...] = total[0:rows, 0:192]
    gk[...] = total[0:rows, 192:384]
    gv[...] = total[0:rows, 384:576]
    for at, out in enumerate(vecs):
        size = out.shape[0]
        out[...] = total[rows + at : rows + at + 1, 0:size].reshape(size)


def final_second_kernel(p0, p1, p2, p3, go, gu):
    total = p0[...].astype(f32) + p1[...].astype(f32) + p2[...].astype(f32) + p3[...].astype(f32)
    go[...] = jnp.transpose(total[:, 0:192])
    gu[...] = total[:, 192:960]


def final_third_kernel(p0, p1, p2, p3, gd):
    total = p0[...].astype(f32) + p1[...].astype(f32) + p2[...].astype(f32) + p3[...].astype(f32)
    gd[...] = jnp.transpose(total)


def plain(kernel, ins, outs, name):
    return pl.pallas_call(
        kernel,
        in_specs=[VMEM] * len(ins),
        out_specs=[VMEM] * len(outs),
        out_shape=outs,
        cost_estimate=cost(1e7, 4e6),
        name=name,
    )(*ins)


def swap(x, axis, bit):
    size = lax.axis_size(axis)
    return lax.ppermute(x, axis, [(i, i ^ bit) for i in range(size)])


def core_swap(x):
    return swap(x, "tensor", 1)


def chip_swap(x):
    return swap(x, "tensor", 2)


def z_from(x, shift):
    size = lax.axis_size("dp")
    return lax.ppermute(x, "dp", [((i + 2 * shift) % size, i) for i in range(size)])


def z_to(x, shift):
    size = lax.axis_size("dp")
    return lax.ppermute(x, "dp", [(i, (i + 2 * shift) % size) for i in range(size)])


def gather_z(shard):
    return [shard] + [z_from(shard, s) for s in (1, 2, 3)]


def after(x, *others):
    return lax.optimization_barrier((x,) + others)[0]


def gather_yx(pieces, last_by_x):
    a = jnp.concatenate(pieces, axis=0)
    a_other = chip_swap(a)
    b = swap(a, "dp", 1)
    b_other = chip_swap(b) if last_by_x else swap(a_other, "dp", 1)
    return [a, b], [a_other, b_other]


def add_low(x, y):
    return (x.astype(f32) + y.astype(f32)).astype(bf16)


def reduce_group(own, other, x_first):
    half = own.shape[0] // 2
    if x_first:
        own = add_low(own, chip_swap(other))
        near = add_low(own[:half], swap(own[half:], "dp", 1))
    else:
        near = add_low(own[:half], swap(own[half:], "dp", 1))
        far = add_low(other[:half], swap(other[half:], "dp", 1))
        near = add_low(near, chip_swap(far))
    rows = half // 4
    return [near[:rows]] + [z_to(near[s * rows : (s + 1) * rows], s) for s in (1, 2, 3)]


def on_device(
    tokens, segments, random_blocks, w_query, w_key, w_value, w_out, w_up, w_down, bias_query, bias_value, bias_out,
    bias_up, bias_down, gain_attn, shift_attn, gain_out, shift_out, cotangent,
):
    dp_size = lax.axis_size("dp")
    fast = dp_size == 8
    length = segments.shape[1]
    half = length // 2
    place = lax.axis_index("dp")
    slot = lax.axis_index("tensor")
    b = jnp.arange(16)
    near = ((place // 2 + b % 4) % 4) * 2 + (place % 2 + b // 4) % 2
    table = jnp.where(b < 8, near if fast else 0, jnp.where(b == 8, slot % 2, slot // 2))
    sc = table.astype(jnp.int32)
    rb = random_blocks.reshape(16, 9)
    rb_other = chip_swap(rb)
    vectors = (bias_query, bias_value, bias_up, bias_out, bias_down, gain_attn, shift_attn, gain_out, shift_out)
    rows = w_query.shape[0]
    if fast:
        blocks1, blocks2, blocks3 = Blocks(8, rows, rows + VEC), Blocks(8, rows, rows), Blocks(8, rows, rows)
        (first,) = plain(
            pack_first_kernel, (w_query, w_key, w_value) + vectors, [sds((rows + VEC, 576), bf16)], "pack_first"
        )
        second, third = plain(
            pack_rest_kernel, (w_out, w_up, w_down), [sds((rows, 960), bf16), sds((rows, 768), bf16)], "pack_rest"
        )
        z1 = gather_z(first)
        g1 = gather_yx(z1, True)
        second = after(second, *z1)
        z2 = gather_z(second)
        g2 = gather_yx(z2, False)
        third = after(third, *z2)
        g3 = gather_yx(gather_z(third), True)
        in1 = g1
    else:
        blocks1 = blocks2 = blocks3 = Blocks(1, D, D)
        gather = lambda x: lax.all_gather(x, "dp", axis=0, tiled=True)
        w1 = gather(jnp.concatenate([w_query, w_key, w_value], axis=1))
        w2 = gather(jnp.concatenate([w_out.T, w_up], axis=1))
        w3 = gather(w_down.T)
        g1, g2, g3 = ([w1], [chip_swap(w1)]), ([w2], [chip_swap(w2)]), ([w3], [chip_swap(w3)])
        lines = [jnp.pad(gather(v).astype(f32), (0, D - dp_size * v.shape[0])) for v in vectors]
        vec = jnp.concatenate([jnp.stack(lines), jnp.zeros((VEC - 9, D), f32)])
        in1 = ([w1, vec], [g1[1][0], chip_swap(vec)])
    count = len(g2[0])

    qaug, kaug = prep(sc, segments, rb, rb_other)
    qkv_a, vec_a = project(blocks1, sc, tokens, qaug, in1[0])
    ctx_a, lse_a = attn_fwd(qkv_a, kaug, 0)
    qkv_b, vec_b = project(blocks1, sc, tokens, qaug, in1[1])
    ctx_b, lse_b = attn_fwd(qkv_b, kaug, 1)

    give, keep = whole(
        functools.partial(out_project_kernel, blocks2, count),
        [sc, ctx_a, ctx_b, *g2[0], *g2[1]],
        [sds((half, D), bf16), sds((half, D), f32)],
        [pltpu.VMEM((D, 256), bf16)] * 2,
        2 * length * D * 512,
        "out_project",
    )
    normal, norm_own, inv = norm_one(sc, keep, core_swap(give), tokens, vec_a)
    norm_oth = core_swap(norm_own)
    act_a_own, act_b_own, sl_a_own, sl_b_own, keep = mlp(blocks2, sc, norm_own, vec_a, vec_b, g2, g3, f32)
    act_a_oth, act_b_oth, sl_a_oth, sl_b_oth, give = mlp(blocks2, sc, norm_oth, vec_a, vec_b, g2, g3, bf16)
    out_own, d_own, d_sum, sums_two = norm_two(sc, keep, core_swap(give), normal, vec_a, cotangent)
    d_oth = core_swap(d_own)

    up_a_own, up_b_own, keep, sums_own = mlp_back(blocks2, sc, d_own, (sl_a_own, sl_b_own), g2, g3, f32)
    up_a_oth, up_b_oth, give, sums_oth = mlp_back(blocks2, sc, d_oth, (sl_a_oth, sl_b_oth), g2, g3, bf16)
    nb3 = blocks3.count * blocks3.stride
    gd_a, gd_b = whole(
        functools.partial(grad_down_kernel, blocks3),
        [sc, d_own, d_oth, act_a_own, act_a_oth, act_b_own, act_b_oth],
        [sds((nb3, 768), bf16)] * 2,
        [pltpu.VMEM((D, D), f32)],
        4 * length * D * D,
        "grad_down",
    )
    d_hid, da_own, sums_one = norm_one_back(sc, keep, core_swap(give), d_sum, normal, inv, vec_a)
    da_oth = core_swap(da_own)
    d_all, dc_a, dc_b = whole(
        functools.partial(d_context_kernel, blocks2, count),
        [sc, da_own, da_oth, *g2[0], *g2[1]],
        [sds((length, D), bf16), sds((length, 256), bf16), sds((length, 256), bf16)],
        [pltpu.VMEM((D, 256), bf16)],
        2 * length * D * 512,
        "d_context",
    )
    gu_a, gu_b = whole(
        functools.partial(grad_up_kernel, blocks2),
        [sc, norm_own, norm_oth, up_a_own, up_a_oth, up_b_own, up_b_oth, d_all, ctx_a, ctx_b],
        [sds((nb3, 960), bf16)] * 2,
        [pltpu.VMEM((D, D), f32)],
        4 * length * D * D,
        "grad_up",
    )
    rep = jnp.concatenate(
        [sums_one[0:1], sums_two[0:1], sums_one[1:3], sums_two[1:3], jnp.zeros((2, D), f32)], axis=0
    )
    rep = rep + core_swap(rep)
    sums_up = sums_own + sums_oth

    dqkv_b = attn_bwd(qkv_b, kaug, ctx_b, lse_b, dc_b, 1)
    nb1 = blocks1.count * blocks1.stride

    def grad_qkv(dqkv, line):
        return whole(
            functools.partial(grad_qkv_kernel, blocks1),
            [sc, tokens, dqkv, sums_up[line : line + 1], rep],
            [sds((nb1, 576), bf16), sds((VEC, D), f32)],
            [pltpu.VMEM((D, D), f32)],
            2 * length * D * D,
            "grad_qkv",
        )

    gq_b, gvec_b = grad_qkv(dqkv_b, 1)
    dqkv_a = attn_bwd(qkv_a, kaug, ctx_a, lse_a, dc_a, 0)
    give, keep = whole(
        functools.partial(d_input_kernel, blocks1, len(g1[0])),
        [sc, dqkv_a, dqkv_b, *g1[0], *g1[1]],
        [sds((half, D), bf16), sds((half, D), f32)],
        [pltpu.VMEM((D, D), bf16)] * 2,
        4 * length * D * D,
        "d_input",
    )
    gq_a, gvec_a = grad_qkv(dqkv_a, 0)
    in_own = keep + core_swap(give).astype(f32) + d_hid

    if fast:
        third = reduce_group(gd_a, gd_b, True)
        second = reduce_group(gu_a, gu_b, False)
        first = reduce_group(gq_a, gq_b, True)
        gvecs = [sds(v.shape, f32) for v in vectors]
        gq, gk, gv, *vec_grads = plain(
            functools.partial(final_first_kernel, rows), first, [sds((rows, 192), f32)] * 3 + gvecs, "final_first"
        )
        go, gu = plain(final_second_kernel, second, [sds((192, rows), f32), sds((rows, 768), f32)], "final_second")
        (gd,) = plain(final_third_kernel, third, [sds((768, rows), f32)], "final_third")
    else:
        scatter = lambda x: lax.psum_scatter(x.astype(f32), "dp", scatter_dimension=0, tiled=True)
        first = scatter(add_low(gq_a, chip_swap(gq_b)))
        gq, gk, gv = first[:, :192], first[:, 192:384], first[:, 384:]
        second = scatter(add_low(gu_a, chip_swap(gu_b)))
        go, gu = second[:, :192].T, second[:, 192:]
        gd = scatter(add_low(gd_a, chip_swap(gd_b))).T
        total = gvec_a + chip_swap(gvec_b)
        total = lax.psum(total, "dp")
        vec_grads = [
            lax.dynamic_slice(total, (i, place * v.shape[0]), (1, v.shape[0]))[0] for i, v in enumerate(vectors)
        ]

    def spread(own):
        over = chip_swap(own)
        mine, other = core_swap(own), core_swap(over)
        return own, mine, over, other

    def assemble(own, mine, over, other, dtype):
        core, chip = slot % 2, slot // 2
        pair = lambda x, y: jnp.where(core == 0, jnp.stack([x, y]), jnp.stack([y, x]))
        here, there = pair(own.astype(dtype), mine.astype(dtype)), pair(over.astype(dtype), other.astype(dtype))
        both = jnp.where(chip == 0, jnp.stack([here, there]), jnp.stack([there, here]))
        return both.reshape(2 * length, D)

    activations = assemble(*spread(out_own), bf16)
    input_grad = assemble(*spread(in_own.astype(bf16)), f32)
    bq, bv, bup, bout, bdown, ga, sa, gout, sout = vec_grads
    return (activations, input_grad, gq, gk, gv, go, gu, gd, bq, bv, bout, bup, bdown, ga, sa, gout, sout)


def solution(mesh):
    placed = (
        P("dp", None),
        P("dp", None),
        P(None, "tensor", None),
        P("dp", "tensor"),
        P("dp", "tensor"),
        P("dp", "tensor"),
        P("tensor", "dp"),
        P("dp", "tensor"),
        P("tensor", "dp"),
        P(("tensor", "dp")),
        P(("tensor", "dp")),
        P("dp"),
        P(("tensor", "dp")),
        P("dp"),
        P("dp"),
        P("dp"),
        P("dp"),
        P("dp"),
        P("dp", None),
    )
    return jax.shard_map(
        on_device,
        mesh=mesh,
        in_specs=placed,
        out_specs=(
            P("dp", None),
            P("dp", None),
            P("dp", "tensor"),
            P("dp", "tensor"),
            P("dp", "tensor"),
            P("tensor", "dp"),
            P("dp", "tensor"),
            P("tensor", "dp"),
            P(("tensor", "dp")),
            P(("tensor", "dp")),
            P("dp"),
            P(("tensor", "dp")),
            P("dp"),
            P("dp"),
            P("dp"),
            P("dp"),
            P("dp"),
        ),
        check_vma=False,
    )
```
